32 devices in a mesh: inner: 4 (over y, x), outer: 8 (over z, core).
Axes of the slice: x: 2, y: 2, z: 4, core: 2. Of those that a mesh axis runs over, the one named last changes fastest.
Arguments:
- points: bfloat16 [8, 16384, 512], P('outer', 'inner'), may hold values from -6 to 6
- bases: bfloat16 [5, 8, 16384, 128], P(None, 'outer', 'inner'), may hold values from -0.09375 to 0.09375
- near_tiles: bfloat16 [8, 3072, 4096], P('outer', 'inner'), may hold values from -0.21875 to 0.21875
- tile_rows: int32 [8, 3072], P('outer', 'inner'), may hold values from 0 to 63, as said below
- tile_cols: int32 [8, 3072], P('outer', 'inner'), may hold values from 0 to 63, as said below
Outputs:
- applied: bfloat16 [8, 16384, 512], P('outer', 'inner')
The draws below stay inside these ranges and needn't reach their ends.
Inputs may be any that keep to these rules, and one draw needn't show every extreme that they name: Each leaf's 768 entries of tile_rows and tile_cols, read together, are distinct pairs (row tile, column tile) of that leaf, sorted by row tile and then column tile; every diagonal pair (a, a) is present, so every row tile has at least one tile. `tile_cols`: read together with tile_rows.
All inputs are finite; a program needn't handle non-finite values.
Results may differ from the reference program's by a relative error of at most 0.0046.
Values sent between devices are 32-bit elements; how exact they have to be, the bound alone decides.
A program may use at most 192 MiB of HBM per device.

```python
import jax
import jax.numpy as jnp
from jax import lax

LEAF = 4096
TILE = 64
RANK = 128
NRHS = 512
NEAR = 12
ROWT = 64
NT_DEV = 768
TILE_SQ = 4096
LEVELS = 5
OUTER_PTS = 16384
INNER_TILES = 3072
N_INNER = 4
N_OUTER = 8


def tile_lists(key):
    base_key = jax.random.fold_in(key, 17)

    def per_leaf(leaf_key):
        off_count = ROWT * (ROWT - 1)
        chosen = jax.random.permutation(leaf_key, off_count)[:NT_DEV - ROWT].astype(jnp.int32)
        row_part = chosen // (ROWT - 1)
        col_part = chosen % (ROWT - 1)
        col_part = col_part + (col_part >= row_part).astype(jnp.int32)
        diagonal = jnp.arange(ROWT, dtype=jnp.int32)
        all_rows = jnp.concatenate([diagonal, row_part])
        all_cols = jnp.concatenate([diagonal, col_part])
        ordering = jnp.argsort(all_rows * ROWT + all_cols, stable=True)
        return (all_rows[ordering], all_cols[ordering])
    leaf_keys = jax.random.split(base_key, N_INNER * N_OUTER)
    row_lists, col_lists = jax.vmap(per_leaf)(leaf_keys)
    return (row_lists.reshape(N_OUTER, INNER_TILES).astype(jnp.int32), col_lists.reshape(N_OUTER, INNER_TILES).astype(jnp.int32))


def draw_tile_rows(key, part):
    return tile_lists(key)[0]


def draw_tile_cols(key, part):
    return tile_lists(key)[1]


def steps_of(own_key, dims, cuts, low, high):
    def one(axis_at, blocks):
        draws = jax.random.uniform(jax.random.fold_in(jax.random.fold_in(own_key, 6), axis_at), (blocks,), jnp.float32, low / len(cuts), high / len(cuts))
        return jnp.repeat(jnp.exp(draws), dims[axis_at] // blocks).reshape((-1,) + (1,) * (len(dims) - axis_at - 1))

    loudness = one(*cuts[0])
    for cut in cuts[1:]:
        loudness = loudness * one(*cut)
    return loudness


def noise(own_key, extent, deviation, most, shards=(), kind=jnp.bfloat16):
    factor_of = steps_of(own_key, extent, shards, -0.22, 0.18) if shards else 1.0
    entries = jax.random.normal(own_key, extent, jnp.float32) * deviation * factor_of
    return jnp.minimum(jnp.maximum(entries, -most), most).astype(kind)


def setup_inputs(seed: int = 0) -> dict:
    arg_keys = jax.random.split(jax.random.key(seed), 6)
    return {
        "points": noise(arg_keys[0], (N_OUTER, OUTER_PTS, NRHS), 1.0, 6.0, ((0, 8), (1, 4))),
        "bases": noise(arg_keys[1], (LEVELS, N_OUTER, OUTER_PTS, RANK), LEAF ** -0.5, 0.09375, ((1, 8), (2, 4))),
        "near_tiles": noise(arg_keys[2], (N_OUTER, INNER_TILES, TILE_SQ), (TILE * NEAR) ** -0.5, 0.21875, ((0, 8), (1, 4))),
        "tile_rows": draw_tile_rows(jax.random.fold_in(arg_keys[5], 71), 0),
        "tile_cols": draw_tile_cols(jax.random.fold_in(arg_keys[5], 71), 0),
    }


def reference(points, bases, near_tiles, tile_rows, tile_cols):
    devices = N_INNER * N_OUTER
    flat_points = points.reshape(devices, LEAF, NRHS)
    flat_bases = bases.reshape(LEVELS, devices, LEAF, RANK)
    flat_tiles = near_tiles.reshape(devices, NT_DEV, TILE, TILE)
    flat_rows = tile_rows.reshape(devices, NT_DEV)
    flat_cols = tile_cols.reshape(devices, NT_DEV)

    def partial_of(leaf_index):
        leaf_bases = flat_bases[:, leaf_index].astype(jnp.float32)
        leaf_points = flat_points[leaf_index].astype(jnp.float32)
        return jnp.einsum("hpr,pb->hrb", leaf_bases, leaf_points, precision=lax.Precision.HIGHEST)

    partial_value = lax.map(partial_of, jnp.arange(devices, dtype=jnp.int32))
    sibling_list = []
    for height in range(LEVELS):
        group_size = 2 ** height
        grouped = jnp.sum(partial_value[:, height].reshape(devices // group_size, group_size, RANK, NRHS), axis=1)
        swapped = grouped.reshape(devices // (2 * group_size), 2, RANK, NRHS)[:, ::-1]
        swapped = swapped.reshape(devices // group_size, RANK, NRHS)
        sibling_list.append(jnp.repeat(swapped, group_size, axis=0))
    coefficients = jnp.stack(sibling_list, axis=1).astype(jnp.bfloat16)

    def apply_leaf(leaf_index):
        by_tile = flat_points[leaf_index].astype(jnp.float32).reshape(ROWT, TILE, NRHS)
        gathered = by_tile[flat_cols[leaf_index]]
        products = jnp.einsum("nij,njb->nib", flat_tiles[leaf_index].astype(jnp.float32), gathered,
                              precision=lax.Precision.HIGHEST)
        near_field = jax.ops.segment_sum(products, flat_rows[leaf_index], num_segments=ROWT).reshape(LEAF, NRHS)
        far_field = jnp.einsum("hpr,hrb->pb", flat_bases[:, leaf_index].astype(jnp.float32),
                               coefficients[leaf_index].astype(jnp.float32), precision=lax.Precision.HIGHEST)
        return (near_field + far_field).astype(jnp.bfloat16)

    applied = lax.map(apply_leaf, jnp.arange(devices, dtype=jnp.int32))
    return applied.reshape(N_OUTER, OUTER_PTS, NRHS)
```

```python
import functools

import jax
import jax.numpy as jnp
from jax import lax
from jax.experimental import pallas as pl
from jax.experimental.pallas import tpu as pltpu
from jax.sharding import PartitionSpec as P

LEAF = 4096
TILE = 64
STRIP_TILES = 8


def swap(block, axis, bit):
    count = lax.axis_size(axis)
    return lax.ppermute(block, axis, [(i, i ^ (1 << bit)) for i in range(count)])


def scatter_half(block, axis, bit):
    side = (lax.axis_index(axis) >> bit) & 1
    half = block.shape[-2] // 2
    low, high = block[..., :half, :], block[..., half:, :]
    kept = jnp.where(side == 0, low, high)
    sent = jnp.where(side == 0, high, low)
    return kept + swap(sent, axis, bit)


def gather_half(block, axis, bit):
    side = (lax.axis_index(axis) >> bit) & 1
    other = swap(block, axis, bit)
    low = jnp.where(side == 0, block, other)
    high = jnp.where(side == 0, other, block)
    return jnp.concatenate([low, high], axis=-2)


def siblings_of(partial_value):
    inner_bits = lax.axis_size("inner").bit_length() - 1
    outer_bits = lax.axis_size("outer").bit_length() - 1
    rhs_count = partial_value.shape[-1]
    upper = partial_value[inner_bits:]
    orders = (list(range(inner_bits)), list(range(inner_bits))[::-1])
    width = rhs_count // 2
    pieces = []
    for at, order in enumerate(orders):
        piece = upper[..., at * width : (at + 1) * width]
        for bit in order:
            piece = scatter_half(piece, "inner", bit)
        pieces.append(piece)
    carried = jnp.concatenate(pieces, axis=-1)
    upper_siblings = []
    for bit in range(outer_bits):
        received = swap(carried, "outer", bit)
        upper_siblings.append(received[0])
        carried = (carried + received)[1:]
    upper = jnp.stack(upper_siblings)
    pieces = []
    for at, order in enumerate(orders):
        piece = upper[..., at * width : (at + 1) * width]
        for bit in order[::-1]:
            piece = gather_half(piece, "inner", bit)
        pieces.append(piece)
    upper = jnp.concatenate(pieces, axis=-1)
    lower = []
    for level in range(inner_bits):
        piece = partial_value[level]
        for bit in range(level):
            piece = scatter_half(piece, "inner", bit)
        piece = swap(piece, "inner", level)
        for bit in range(level)[::-1]:
            piece = gather_half(piece, "inner", bit)
        lower.append(piece)
    return jnp.concatenate([jnp.stack(lower), upper], axis=0)


def relayout_kernel(tiles_ref, out_ref, wide):
    count = tiles_ref.shape[0]
    lines = tiles_ref.shape[1] // 128
    for m in range(lines):
        wide[pl.ds(m, count, stride=lines), :] = tiles_ref[:, m * 128 : (m + 1) * 128].astype(
            jnp.float32
        )
    out_ref[...] = wide[...].astype(jnp.bfloat16)


def relayout(tiles):
    total, square = tiles.shape
    count = next(c for c in (64, 32, 16, total) if total % c == 0)
    lines = square // 128
    return pl.pallas_call(
        relayout_kernel,
        grid=(total // count,),
        in_specs=[pl.BlockSpec((count, square), lambda i: (i, 0))],
        out_specs=pl.BlockSpec((count * lines, 128), lambda i: (i, 0)),
        out_shape=jax.ShapeDtypeStruct((total * lines, 128), jnp.bfloat16),
        scratch_shapes=[pltpu.VMEM((count * lines, 128), jnp.float32)],
        cost_estimate=pl.CostEstimate(
            flops=0, bytes_accessed=total * square * 8, transcendentals=0
        ),
        name="relayout",
    )(tiles)


def near_kernel(
    first, per_strip, rows_ref, cols_ref, starts_ref, lines_ref, points_ref, *rest
):
    out_ref, dense, woven = rest[-3:]
    strip = pl.program_id(0) + first
    half = TILE // 2
    last = rows_ref.shape[0] - 1

    @pl.when(pl.program_id(0) == 0)
    def _():
        dense[...] = jnp.zeros_like(dense)

    lane_side = lax.broadcasted_iota(jnp.int32, (half, 128), 1) // TILE
    begin, end = starts_ref[strip], starts_ref[strip + 1]
    batch = 4

    def place(step, carry):
        for k in range(batch):
            at = begin + step * batch + k
            n = jnp.minimum(at, last)
            a = jnp.minimum(jnp.maximum(rows_ref[n] - strip * per_strip, 0), per_strip - 1)
            c = cols_ref[n]
            side = c % 2
            target = jnp.where(at < end, side, 2)
            z = lines_ref[pl.ds(pl.multiple_of(n * half, half), half), :].astype(jnp.float32)
            top = pltpu.roll(z, side * TILE, 1).astype(jnp.bfloat16)
            bottom = pltpu.roll(z, (1 - side) * TILE, 1).astype(jnp.bfloat16)
            row = pl.multiple_of(a * TILE, TILE)
            lane = pl.multiple_of((c // 2) * 128, 128)
            hit = lane_side == target
            dense[pl.ds(row, half), pl.ds(lane, 128)] = jnp.where(
                hit, top, dense[pl.ds(row, half), pl.ds(lane, 128)]
            )
            low = pl.multiple_of(row + half, half)
            dense[pl.ds(low, half), pl.ds(lane, 128)] = jnp.where(
                hit, bottom, dense[pl.ds(low, half), pl.ds(lane, 128)]
            )
        return carry

    lax.fori_loop(0, (end - begin + batch - 1) // batch, place, 0)
    product = jnp.dot(dense[...], points_ref[...], preferred_element_type=jnp.float32)
    dense[...] = jnp.zeros_like(dense)
    for at in range(product.shape[1] // 128):
        lanes = slice(at * 128, (at + 1) * 128)
        for a in range(per_strip):
            base = a * TILE
            woven[pl.ds(base, half, stride=2), :] = product[base : base + half, lanes]
            woven[pl.ds(base + 1, half, stride=2), :] = product[base + half : base + TILE, lanes]
        out_ref[:, lanes] = woven[...]


def near_part(rows, cols, starts, lines, points, near, first, count):
    leaf, rhs_count = points.shape
    per_strip = STRIP_TILES
    height = per_strip * TILE
    in_specs = [
        pl.BlockSpec(lines.shape, lambda i, *_: (0, 0), pipeline_mode=pl.Buffered(1)),
        pl.BlockSpec(points.shape, lambda i, *_: (0, 0), pipeline_mode=pl.Buffered(1)),
    ]
    operands = [lines, points]
    aliases = {}
    if near is not None:
        in_specs.append(pl.BlockSpec(memory_space=pl.ANY))
        operands.append(near)
        aliases = {5: 0}
    return pl.pallas_call(
        functools.partial(near_kernel, first, per_strip),
        grid_spec=pltpu.PrefetchScalarGridSpec(
            num_scalar_prefetch=3,
            grid=(count,),
            in_specs=in_specs,
            out_specs=pl.BlockSpec((height, rhs_count), lambda i, *_: (i + first, 0)),
            scratch_shapes=[
                pltpu.VMEM((height, leaf), jnp.bfloat16),
                pltpu.VMEM((height, 128), jnp.float32),
            ],
        ),
        out_shape=jax.ShapeDtypeStruct((leaf, rhs_count), jnp.float32),
        input_output_aliases=aliases,
        compiler_params=pltpu.CompilerParams(vmem_limit_bytes=40 << 20),
        cost_estimate=pl.CostEstimate(
            flops=2 * count * height * leaf * rhs_count,
            bytes_accessed=lines.size * 2 + points.size * 2 + count * height * rhs_count * 4,
            transcendentals=0,
        ),
        name="near_field",
    )(rows, cols, starts, *operands)


def far_kernel(bases_ref, sibling_ref, near_ref, out_ref, coef_ref):
    @pl.when(pl.program_id(0) == 0)
    def _():
        coef_ref[...] = sibling_ref[...].astype(jnp.bfloat16)

    total = near_ref[...]
    for h in range(bases_ref.shape[0]):
        total = total + jnp.dot(
            bases_ref[h, 0], coef_ref[h], preferred_element_type=jnp.float32
        )
    out_ref[0] = total.astype(jnp.bfloat16)


def far_apply(bases, siblings, near):
    levels, _, leaf, rank = bases.shape
    rhs_count = near.shape[1]
    height = 512
    return pl.pallas_call(
        far_kernel,
        grid=(leaf // height,),
        in_specs=[
            pl.BlockSpec((levels, 1, height, rank), lambda i: (0, 0, i, 0)),
            pl.BlockSpec(siblings.shape, lambda i: (0, 0, 0)),
            pl.BlockSpec((height, rhs_count), lambda i: (i, 0)),
        ],
        out_specs=pl.BlockSpec((1, height, rhs_count), lambda i: (0, i, 0)),
        out_shape=jax.ShapeDtypeStruct((1, leaf, rhs_count), jnp.bfloat16),
        scratch_shapes=[pltpu.VMEM(siblings.shape, jnp.bfloat16)],
        name="far_field",
    )(bases, siblings, near)


def local(points, bases, near_tiles, tile_rows, tile_cols):
    local_points = points[0]
    partial_value = jnp.einsum(
        "hpr,pb->hrb", bases[:, 0], local_points, preferred_element_type=jnp.float32
    )
    siblings = siblings_of(partial_value)
    rows, cols = tile_rows[0], tile_cols[0]
    strips = LEAF // (TILE * STRIP_TILES)
    bounds = jnp.arange(strips + 1, dtype=jnp.int32) * STRIP_TILES
    starts = jnp.sum(rows[None, :] < bounds[:, None], axis=1, dtype=jnp.int32)
    lines = relayout(near_tiles[0])
    near = None
    parts = 4
    step = strips // parts
    for part in range(parts):
        near = near_part(rows, cols, starts, lines, local_points, near, part * step, step)
    return far_apply(bases, siblings, near)


def solution(mesh):
    placed = (
        P("outer", "inner", None),
        P(None, "outer", "inner", None),
        P("outer", "inner", None),
        P("outer", "inner"),
        P("outer", "inner"),
    )
    return jax.shard_map(
        local, mesh=mesh, in_specs=placed, out_specs=P("outer", "inner", None), check_vma=False
    )
```

```python
import functools

import jax
import jax.numpy as jnp
from jax import lax
from jax.experimental import pallas as pl
from jax.experimental.pallas import tpu as pltpu
from jax.sharding import PartitionSpec as P


LEAF = 4096
TILE = 64
STRIP_TILES = 8
PARTS = 8


def swap(block, axis, bit):
    count = lax.axis_size(axis)
    return lax.ppermute(block, axis, [(i, i ^ (1 << bit)) for i in range(count)])


def scatter_half(block, axis, bit):
    side = (lax.axis_index(axis) >> bit) & 1
    half = block.shape[-2] // 2
    low, high = block[..., :half, :], block[..., half:, :]
    kept = jnp.where(side == 0, low, high)
    sent = jnp.where(side == 0, high, low)
    return kept + swap(sent, axis, bit)


def gather_half(block, axis, bit):
    side = (lax.axis_index(axis) >> bit) & 1
    other = swap(block, axis, bit)
    low = jnp.where(side == 0, block, other)
    high = jnp.where(side == 0, other, block)
    return jnp.concatenate([low, high], axis=-2)


def siblings_of(partial_value):
    inner_bits = lax.axis_size("inner").bit_length() - 1
    outer_bits = lax.axis_size("outer").bit_length() - 1
    rhs_count = partial_value.shape[-1]
    upper = partial_value[inner_bits:]
    orders = (list(range(inner_bits)), list(range(inner_bits))[::-1])
    width = rhs_count // 2
    pieces = []
    for at, order in enumerate(orders):
        piece = upper[..., at * width : (at + 1) * width]
        for bit in order:
            piece = scatter_half(piece, "inner", bit)
        pieces.append(piece)
    carried = jnp.concatenate(pieces, axis=-1)
    upper_siblings = []
    for bit in range(outer_bits):
        received = swap(carried, "outer", bit)
        upper_siblings.append(received[0])
        carried = (carried + received)[1:]
    upper = jnp.stack(upper_siblings)
    pieces = []
    for at, order in enumerate(orders):
        piece = upper[..., at * width : (at + 1) * width]
        for bit in order[::-1]:
            piece = gather_half(piece, "inner", bit)
        pieces.append(piece)
    upper = jnp.concatenate(pieces, axis=-1)
    lower = []
    for level in range(inner_bits):
        piece = partial_value[level]
        for bit in range(level):
            piece = scatter_half(piece, "inner", bit)
        piece = swap(piece, "inner", level)
        for bit in range(level)[::-1]:
            piece = gather_half(piece, "inner", bit)
        lower.append(piece)
    return jnp.concatenate([jnp.stack(lower), upper], axis=0)


def relayout_kernel(tiles_ref, out_ref):
    count, square = tiles_ref.shape
    lines = square // 128
    z = tiles_ref[...].astype(jnp.float32).reshape(count, lines, 128)
    turned = pltpu.roll(z, TILE, 2)
    first = lax.broadcasted_iota(jnp.int32, z.shape, 2) < TILE
    out_ref[:, :lines, :] = jnp.where(first, z, turned).astype(jnp.bfloat16)
    out_ref[:, lines:, :] = jnp.where(first, turned, z).astype(jnp.bfloat16)


def relayout(tiles):
    total, square = tiles.shape
    count = next(c for c in (64, 32, 16, total) if total % c == 0)
    lines = square // 128
    return pl.pallas_call(
        relayout_kernel,
        grid=(total // count,),
        in_specs=[pl.BlockSpec((count, square), lambda i: (i, 0))],
        out_specs=pl.BlockSpec((count, 2 * lines, 128), lambda i: (i, 0, 0)),
        out_shape=jax.ShapeDtypeStruct((total, 2 * lines, 128), jnp.bfloat16),
        cost_estimate=pl.CostEstimate(
            flops=0, bytes_accessed=total * square * 8, transcendentals=0
        ),
        name="relayout",
    )(tiles)


def near_kernel(
    first, per_strip, rows_ref, cols_ref, starts_ref, lines_ref, points_ref, *rest
):
    out_ref, dense, woven, sides = rest[-4:]
    strip = pl.program_id(0) + first
    half = TILE // 2
    last = rows_ref.shape[0] - 1

    dense[...] = jnp.zeros_like(dense)
    lane_side = lax.broadcasted_iota(jnp.int32, (TILE, 128), 1) // TILE
    for side in range(3):
        sides[side] = jnp.where(lane_side == side, 1.0, 0.0).astype(jnp.bfloat16)
    begin, end = starts_ref[strip], starts_ref[strip + 1]
    batch = 4

    def place(step, carry):
        for k in range(batch):
            at = begin + step * batch + k
            n = jnp.minimum(at, last)
            c = cols_ref[n]
            keep = sides[jnp.where(at < end, c & 1, 2)]
            row = pl.multiple_of(rows_ref[n], TILE)
            lane = pl.multiple_of(lax.shift_right_logical(c, 1) * 128, 128)
            spot = (pl.ds(row, TILE), pl.ds(lane, 128))
            dense[spot] = dense[spot] + lines_ref[n] * keep
        return carry

    lax.fori_loop(0, (end - begin + batch - 1) // batch, place, 0)
    product = jnp.dot(dense[...], points_ref[...], preferred_element_type=jnp.float32)
    for at in range(product.shape[1] // 128):
        lanes = slice(at * 128, (at + 1) * 128)
        for a in range(per_strip):
            base = a * TILE
            woven[pl.ds(base, half, stride=2), :] = product[base : base + half, lanes]
            woven[pl.ds(base + 1, half, stride=2), :] = product[base + half : base + TILE, lanes]
        out_ref[:, lanes] = woven[...]


def near_part(rows, cols, starts, lines, points, near, first, count):
    leaf, rhs_count = points.shape
    per_strip = STRIP_TILES
    height = per_strip * TILE
    in_specs = [
        pl.BlockSpec(memory_space=pltpu.VMEM),
        pl.BlockSpec(memory_space=pltpu.VMEM),
    ]
    operands = [lines, points]
    aliases = {}
    if near is not None:
        in_specs.append(pl.BlockSpec(memory_space=pl.ANY))
        operands.append(near)
        aliases = {5: 0}
    return pl.pallas_call(
        functools.partial(near_kernel, first, per_strip),
        grid_spec=pltpu.PrefetchScalarGridSpec(
            num_scalar_prefetch=3,
            grid=(count,),
            in_specs=in_specs,
            out_specs=pl.BlockSpec((height, rhs_count), lambda i, *_: (i + first, 0)),
            scratch_shapes=[
                pltpu.VMEM((height, leaf), jnp.bfloat16),
                pltpu.VMEM((height, 128), jnp.float32),
                pltpu.VMEM((3, TILE, 128), jnp.bfloat16),
            ],
        ),
        out_shape=jax.ShapeDtypeStruct((leaf, rhs_count), jnp.float32),
        input_output_aliases=aliases,
        compiler_params=pltpu.CompilerParams(vmem_limit_bytes=12 << 20),
        cost_estimate=pl.CostEstimate(
            flops=2 * count * height * leaf * rhs_count,
            bytes_accessed=lines.size * 2 + points.size * 2 + count * height * rhs_count * 4,
            transcendentals=0,
        ),
        name="near_field",
    )(rows, cols, starts, *operands)


def far_kernel(bases_ref, sibling_ref, near_ref, out_ref, coef_ref):
    @pl.when(pl.program_id(0) == 0)
    def _():
        coef_ref[...] = sibling_ref[...].astype(jnp.bfloat16)

    levels, rank = sibling_ref.shape[:2]
    wide = jnp.concatenate([bases_ref[h, 0] for h in range(levels)], axis=1)
    coefs = coef_ref[...].reshape(levels * rank, coef_ref.shape[2])
    height = out_ref.shape[1]
    at = pl.ds(pl.multiple_of(pl.program_id(0) * height, height), height)
    total = near_ref[at, :] + jnp.dot(wide, coefs, preferred_element_type=jnp.float32)
    out_ref[0] = total.astype(jnp.bfloat16)


def far_apply(bases, siblings, near):
    levels, _, leaf, rank = bases.shape
    rhs_count = near.shape[1]
    height = 512
    return pl.pallas_call(
        far_kernel,
        grid=(leaf // height,),
        in_specs=[
            pl.BlockSpec((levels, 1, height, rank), lambda i: (0, 0, i, 0)),
            pl.BlockSpec(siblings.shape, lambda i: (0, 0, 0)),
            pl.BlockSpec(memory_space=pltpu.VMEM),
        ],
        out_specs=pl.BlockSpec((1, height, rhs_count), lambda i: (0, i, 0)),
        out_shape=jax.ShapeDtypeStruct((1, leaf, rhs_count), jnp.bfloat16),
        scratch_shapes=[pltpu.VMEM(siblings.shape, jnp.bfloat16)],
        compiler_params=pltpu.CompilerParams(vmem_limit_bytes=12 << 20),
        name="far_field",
    )(bases, siblings, near)


def local(points, bases, near_tiles, tile_rows, tile_cols):
    local_points = points[0]
    partial_value = jnp.einsum(
        "hpr,pb->hrb", bases[:, 0], local_points, preferred_element_type=jnp.float32
    )
    siblings = siblings_of(partial_value)
    rows, cols = tile_rows[0], tile_cols[0]
    strips = LEAF // (TILE * STRIP_TILES)
    bounds = jnp.arange(strips + 1, dtype=jnp.int32) * STRIP_TILES
    starts = jnp.sum(rows[None, :] < bounds[:, None], axis=1, dtype=jnp.int32)
    lines = relayout(near_tiles[0])
    rows = rows % STRIP_TILES * TILE
    near = None
    step = strips // PARTS
    for part in range(PARTS):
        near = near_part(rows, cols, starts, lines, local_points, near, part * step, step)
    return far_apply(bases, siblings, near)


def solution(mesh):
    placed = (
        P("outer", "inner", None),
        P(None, "outer", "inner", None),
        P("outer", "inner", None),
        P("outer", "inner"),
        P("outer", "inner"),
    )

    return jax.shard_map(
        local, mesh=mesh, in_specs=placed, out_specs=P("outer", "inner", None), check_vma=False
    )
```
